256 devices in a mesh: seq: 32 (over z_lo, y, core), head: 8 (over z_hi, x).
Axes of the slice: x: 4, y: 4, z: 8 (z_hi: 2, z_lo: 4; z = z_hi * 4 + z_lo), core: 2. Of those that a mesh axis runs over, the one named last changes fastest.
Arguments:
- fast_q: bfloat16 [8192, 4096], P('seq', 'head'), may hold values from -6 to 6
- fast_k: bfloat16 [8192, 4096], P('seq', 'head'), may hold values from -6 to 6
- fast_v: bfloat16 [8192, 4096], P('seq', 'head'), may hold values from -6 to 6
- rates: float32 [8, 8192], P('head', 'seq'), may hold values from 0.02 to 1
- w_gate: bfloat16 [8, 512, 512], P('head'), may hold values from -0.25 to 0.25
- w_up: bfloat16 [8, 512, 512], P('head'), may hold values from -0.25 to 0.25
- w_down: bfloat16 [8, 512, 512], P('head'), may hold values from -0.25 to 0.25
- w_out: bfloat16 [4096, 5120], P('head'), may hold values from -0.09375 to 0.09375
- att_q: bfloat16 [8192, 5120], P('seq', 'head'), may hold values from -5 to 5
- att_k: bfloat16 [8192, 5120], P('seq', 'head'), may hold values from -5 to 5
- att_v: bfloat16 [8192, 5120], P('seq', 'head'), may hold values from -6 to 6
Outputs:
- mixed: bfloat16 [8192, 5120], P('seq', 'head')
- final_weights: bfloat16 [3, 8, 512, 512], P(None, 'head', 'seq')
The draws below stay inside these ranges and needn't reach their ends.
All inputs are finite; a program needn't handle non-finite values.
Results may differ from the reference program's by a relative error of at most 0.022.
Values may be sent and summed in bfloat16 or wider, within the bound.
No kernel may reach another device: no remote copies, remote signals or barrier semaphores. Data moves between devices by JAX's collectives and lax.ppermute only.
A program may use at most 64 MiB of HBM per device.

```python
import math
import jax
import jax.numpy as jnp
from jax import lax

HEADS = 8
DH = 512
AHEADS = 40
AD = 128
SPANS = 2
NS_STEPS = 2
TOK_DEV = 256
D = 5120
TOKENS = 8192
WINDOW = 256
N_HEAD = 8


def attention_pair(key):
    base = jax.random.fold_in(key, 4242)
    queries = jnp.clip(1.5 * jax.random.normal(jax.random.fold_in(base, 1), (TOKENS, D), jnp.float32), -5.0, 5.0)
    keys_drawn = jnp.clip(1.5 * jax.random.normal(jax.random.fold_in(base, 2), (TOKENS, D), jnp.float32), -5.0, 5.0)
    return (queries, keys_drawn)


def draw_att_q(key, part):
    return attention_pair(key)[0].astype(jnp.bfloat16)


def draw_att_k(key, part):
    return attention_pair(key)[1].astype(jnp.bfloat16)


def levels(rng, extent, cuts, low, high):
    def one(axis_at, shards_of):
        heights = jax.random.uniform(jax.random.fold_in(jax.random.fold_in(rng, 6), axis_at), (shards_of,), jnp.float32, low / len(cuts), high / len(cuts))
        return jnp.repeat(jnp.exp(heights), extent[axis_at] // shards_of).reshape((-1,) + (1,) * (len(extent) - axis_at - 1))

    factor_of = one(*cuts[0])
    for cut in cuts[1:]:
        factor_of = factor_of * one(*cut)
    return factor_of


def noise(own_key, extent, width, limit, cuts=(), held_as=jnp.bfloat16):
    drawn = width * jax.random.normal(own_key, extent, jnp.float32)
    if cuts:
        drawn = drawn * levels(own_key, extent, cuts, -0.22, 0.18)
    return jnp.clip(drawn, -limit, limit).astype(held_as)


def setup_inputs(seed: int = 0) -> dict:
    splits = jax.random.split(jax.random.key(seed), 12)
    fast_q = noise(splits[0], (TOKENS, HEADS * DH), 1.0, 6.0, ((0, 32), (1, 8)))
    fast_k = noise(splits[1], (TOKENS, HEADS * DH), 1.0, 6.0, ((0, 32), (1, 8)))
    fast_v = noise(splits[2], (TOKENS, HEADS * DH), 1.0, 6.0, ((0, 32), (1, 8)))
    rates = jnp.clip(jnp.exp(math.log(1.0) - 3.912023 * jax.random.uniform(splits[3], (HEADS, TOKENS), jnp.float32) ** levels(splits[3], (HEADS, TOKENS), ((0, 8), (1, 32)), -0.2, 0.2)), 0.02, 1.0)
    w_gate = noise(splits[4], (HEADS, DH, DH), DH ** -0.5, 0.25, ((0, 8),))
    w_up = noise(splits[5], (HEADS, DH, DH), DH ** -0.5, 0.25, ((0, 8),))
    w_down = noise(splits[6], (HEADS, DH, DH), DH ** -0.5, 0.25, ((0, 8),))
    w_out = noise(splits[7], (HEADS * DH, D), (HEADS * DH) ** -0.5, 0.09375, ((0, 8),))
    att_q = draw_att_q(jax.random.fold_in(splits[11], 71), 0)
    att_k = draw_att_k(jax.random.fold_in(splits[11], 71), 0)
    att_v = noise(splits[10], (TOKENS, D), 1.0, 6.0, ((0, 32), (1, 8)))
    return {"fast_q": fast_q, "fast_k": fast_k, "fast_v": fast_v, "rates": rates, "w_gate": w_gate, "w_up": w_up, "w_down": w_down, "w_out": w_out, "att_q": att_q, "att_k": att_k, "att_v": att_v}


NEWTON_COEFFS = (3.4445, -4.775, 2.0315)

def silu_slope(values):
    sigmoid_val = jax.nn.sigmoid(values)
    return sigmoid_val * (1.0 + values * (1.0 - sigmoid_val))

def product(pattern, left_op, right_op):
    return jnp.einsum(pattern, left_op.astype(jnp.float32), right_op.astype(jnp.float32))

def fast_apply(weights, queries):
    w_first, w_second, w_third = weights
    gate_pre = product('nhi,hij->nhj', queries, w_first)
    up_pre = product('nhi,hij->nhj', queries, w_second)
    activated = (jax.nn.silu(gate_pre) * up_pre).astype(jnp.bfloat16)
    output = product('nhj,hjk->nhk', activated, w_third)
    factor = lax.rsqrt(lax.optimization_barrier(jnp.mean(output * output, axis=-1, keepdims=True)) + 1e-06)
    return (output * factor).astype(jnp.bfloat16)

def gradients(weights, keys_in, values_in, rate_rows):
    w_first, w_second, w_third = weights
    gate_pre = product('nhi,hij->nhj', keys_in, w_first)
    up_pre = product('nhi,hij->nhj', keys_in, w_second)
    activated = (jax.nn.silu(gate_pre) * up_pre).astype(jnp.bfloat16)
    weighted = (rate_rows[:, :, None] * values_in.astype(jnp.float32)).astype(jnp.bfloat16)
    grad_third = -product('nhj,nhk->hjk', activated, weighted)
    back = -product('nhk,hjk->nhj', weighted, w_third)
    up_in = (back * jax.nn.silu(gate_pre)).astype(jnp.bfloat16)
    gate_in = (back * up_pre * silu_slope(gate_pre)).astype(jnp.bfloat16)
    grad_first = product('nhi,nhj->hij', keys_in, gate_in)
    grad_second = product('nhi,nhj->hij', keys_in, up_in)
    return (grad_first, grad_second, grad_third)

def scale_down(summed):
    squares = lax.optimization_barrier(jnp.sum(summed * summed, axis=(1, 2)))
    return (summed / jnp.sqrt(squares + 1e-06)[:, None, None]).astype(jnp.bfloat16)

def newton_schulz(matrix):
    first, second, third = NEWTON_COEFFS
    for iteration in range(NS_STEPS):
        gram = product('mij,mkj->mik', matrix, matrix).astype(jnp.bfloat16)
        square = product('mij,mjk->mik', gram, gram)
        poly = (second * gram.astype(jnp.float32) + third * square).astype(jnp.bfloat16)
        matrix = (first * matrix.astype(jnp.float32) + product('mij,mjk->mik', poly, matrix)).astype(jnp.bfloat16)
    return matrix

def renorm(weight, ortho):
    unmoved = weight.astype(jnp.float32)
    moved = unmoved - ortho.astype(jnp.float32)
    target = jnp.sqrt(lax.optimization_barrier(jnp.sum(unmoved * unmoved, axis=1, keepdims=True)) + 1e-06)
    current = jnp.sqrt(lax.optimization_barrier(jnp.sum(moved * moved, axis=1, keepdims=True)) + 1e-06)
    return (moved * (target / current)).astype(jnp.bfloat16)

def attend(queries, keys_all, values_all, offset, window):
    block = queries.shape[0]
    scores = product('qhd,khd->hqk', queries, keys_all) * queries.shape[-1] ** (-0.5)
    query_pos = offset + lax.broadcasted_iota(jnp.int32, (block, 2 * block), 0)
    key_pos = offset - block + lax.broadcasted_iota(jnp.int32, (block, 2 * block), 1)
    allowed = (key_pos <= query_pos) & (key_pos > query_pos - window) & (key_pos >= 0)
    scores = jnp.where(allowed[None], scores, -1e+30)
    row_max = lax.optimization_barrier(jnp.max(scores, axis=-1, keepdims=True))
    exp_scores = jnp.exp(scores - row_max)
    probs = (exp_scores / lax.optimization_barrier(jnp.sum(exp_scores, axis=-1, keepdims=True))).astype(jnp.bfloat16)
    return product('hqk,khd->qhd', probs, values_all)

def reference(fast_q, fast_k, fast_v, rates, w_gate, w_up, w_down, w_out, att_q, att_k, att_v):
    length = TOKENS // SPANS
    queries = fast_q.reshape(TOKENS, HEADS, DH)
    keys_fast = fast_k.reshape(TOKENS, HEADS, DH)
    values_fast = fast_v.reshape(TOKENS, HEADS, DH)
    weights = (w_gate, w_up, w_down)
    results = []
    for span in range(SPANS):
        lower = span * length
        upper = lower + length
        results.append(fast_apply(weights, queries[lower:upper]))
        grads = gradients(weights, keys_fast[lower:upper], values_fast[lower:upper], rates[:, lower:upper].T)
        ortho = newton_schulz(scale_down(jnp.concatenate(grads, axis=0)))
        pieces = ortho.reshape(3, HEADS, DH, DH)
        weights = tuple((renorm(weights[member], pieces[member]) for member in range(3)))
    final_weights = jnp.stack(weights, axis=0)
    fast_rows = jnp.concatenate(results, axis=0).reshape(TOKENS, HEADS * DH)
    share = HEADS * DH // N_HEAD
    fast_sum = jnp.zeros((TOKENS, D), jnp.float32)
    for group_id in range(N_HEAD):
        partial_out = jnp.dot(fast_rows[:, group_id * share:(group_id + 1) * share], w_out[group_id * share:(group_id + 1) * share], preferred_element_type=jnp.float32).astype(jnp.bfloat16)
        fast_sum = fast_sum + lax.optimization_barrier(partial_out).astype(jnp.float32)
    queries_att = att_q.reshape(TOKENS, AHEADS, AD)
    padding = jnp.zeros((TOK_DEV, AHEADS, AD), jnp.bfloat16)
    keys_pad = jnp.concatenate([padding, att_k.reshape(TOKENS, AHEADS, AD)], axis=0)
    values_pad = jnp.concatenate([padding, att_v.reshape(TOKENS, AHEADS, AD)], axis=0)

    def one_block(block_id):
        offset = (block_id * TOK_DEV).astype(jnp.int32)
        query_block = lax.dynamic_slice_in_dim(queries_att, offset, TOK_DEV, 0)
        key_block = lax.dynamic_slice_in_dim(keys_pad, offset, 2 * TOK_DEV, 0)
        value_block = lax.dynamic_slice_in_dim(values_pad, offset, 2 * TOK_DEV, 0)
        return attend(query_block, key_block, value_block, offset, WINDOW)
    attended = lax.map(one_block, jnp.arange(TOKENS // TOK_DEV, dtype=jnp.int32))
    attended = attended.reshape(TOKENS, D)
    return ((attended + fast_sum).astype(jnp.bfloat16), final_weights)
```

```python
import functools

import jax
import jax.numpy as jnp
from jax import lax
from jax.experimental import pallas as pl
from jax.experimental.pallas import tpu as pltpu
from jax.sharding import Mesh
from jax.sharding import PartitionSpec as P

AD = 128
NS_STEPS = 2
NEWTON_COEFFS = (3.4445, -4.775, 2.0315)
SEQ = ("span", "row", "y", "core")
CHIPS = ("row", "y")
HEAD = ("head_0", "head_1")
F32 = jnp.float32
BF16 = jnp.bfloat16


VMEM = pl.BlockSpec(memory_space=pltpu.VMEM)
SMEM = pl.BlockSpec(memory_space=pltpu.SMEM)


def nn(a, b):
    return lax.dot_general(a, b, (((1,), (0,)), ((), ())), preferred_element_type=F32)


def nt(a, b):
    return lax.dot_general(a, b, (((1,), (1,)), ((), ())), preferred_element_type=F32)


def tn(a, b):
    return lax.dot_general(a, b, (((0,), (0,)), ((), ())), preferred_element_type=F32)


def call(kernel, outs, args, scratch=(), smem=0):
    return pl.pallas_call(
        kernel,
        out_shape=outs,
        in_specs=[SMEM] * smem + [VMEM] * (len(args) - smem),
        out_specs=jax.tree.map(lambda _: VMEM, outs),
        scratch_shapes=scratch,
    )(*args)


def gradients_kernel(blocks, core_ref, k_ref, v_ref, rate_ref, wg_ref, wu_ref, wd_ref, own_ref, far_ref):
    core = core_ref[0]
    k = k_ref[...]
    weighted = (rate_ref[...] * v_ref[...].astype(F32)).astype(BF16)
    x = nn(k, wg_ref[0])
    u = nn(k, wu_ref[0])
    sig = jax.nn.sigmoid(x)
    silu = x * sig
    act = (silu * u).astype(BF16)
    back = -nt(weighted, wd_ref[0])
    up_in = (back * silu).astype(BF16)
    gate_in = (back * u * (sig * (1.0 + x * (1.0 - sig)))).astype(BF16)
    half = k.shape[1] // 2
    step = half // blocks
    neg_act = -act
    for m, (left, right) in enumerate(((k, gate_in), (k, up_in), (neg_act, weighted))):
        for h in range(2):
            g = tn(left[:, h * half : (h + 1) * half], right).astype(BF16)

            @pl.when(core == h)
            def _():
                for j in range(blocks):
                    own_ref[j, m] = g[j * step : (j + 1) * step]

            @pl.when(core != h)
            def _():
                for j in range(blocks):
                    far_ref[j, m] = g[j * step : (j + 1) * step]


def gradients(core, k, v, rate, weights, blocks):
    features = k.shape[1]
    shape = jax.ShapeDtypeStruct((blocks, 3, features // 2 // blocks, features), BF16)
    return call(
        functools.partial(gradients_kernel, blocks), (shape, shape), (core, k, v, rate, *weights), smem=1
    )


def orthogonal(g):
    first, second, third = NEWTON_COEFFS
    wide = g.astype(F32)
    x = (wide / jnp.sqrt(jnp.sum(wide * wide) + 1e-6)).astype(BF16)
    for _ in range(NS_STEPS):
        gram = nt(x, x).astype(BF16)
        poly = (second * gram.astype(F32) + third * nn(gram, gram)).astype(BF16)
        x = (first * x.astype(F32) + nn(poly, x)).astype(BF16)
    return x


def moved_weight(w, x):
    w = w.astype(F32)
    moved = w - x.astype(F32)
    target = jnp.sqrt(jnp.sum(w * w, axis=0, keepdims=True) + 1e-6)
    current = jnp.sqrt(jnp.sum(moved * moved, axis=0, keepdims=True) + 1e-6)
    return (moved * (target / current)).astype(BF16)


def assembled(core, own_ref, far_ref, m, g_ref):
    blocks, _, step, features = own_ref.shape
    half = blocks * step
    for j in range(blocks):
        g_ref[pl.ds(pl.multiple_of(core * half + j * step, step), step), :] = own_ref[j, m]
        g_ref[pl.ds(pl.multiple_of((1 - core) * half + j * step, step), step), :] = far_ref[j, m]
    return g_ref[...]


def update_kernel(core_ref, own_ref, far_ref, wg_ref, wu_ref, wd_ref, og_ref, ou_ref, od_ref, g_ref):
    core = core_ref[0]
    for m, (w_ref, o_ref) in enumerate(((wg_ref, og_ref), (wu_ref, ou_ref), (wd_ref, od_ref))):
        x = orthogonal(assembled(core, own_ref, far_ref, m, g_ref))
        o_ref[0] = moved_weight(w_ref[0], x)


def update(core, own, far, weights):
    shape = jax.ShapeDtypeStruct(weights[0].shape, BF16)
    return call(
        update_kernel,
        (shape,) * 3,
        (core, own, far, *weights),
        scratch=[pltpu.VMEM(weights[0].shape[1:], BF16)],
        smem=1,
    )


def last_kernel(core_ref, seat_ref, own_ref, far_ref, wg_ref, wu_ref, wd_ref, mine_ref, peer_ref, g_ref):
    core = core_ref[0]
    seat = seat_ref[0]
    share = mine_ref.shape[1]
    half = g_ref.shape[0] // 2
    for m, w_ref in enumerate((wg_ref, wu_ref, wd_ref)):
        x = orthogonal(assembled(core, own_ref, far_ref, m, g_ref))
        g_ref[...] = moved_weight(w_ref[0], x)
        peer_ref[m] = g_ref[pl.ds(pl.multiple_of(seat * share, share), share), :]
        mine_ref[m] = g_ref[pl.ds(pl.multiple_of(half + seat * share, share), share), :]


def last_update(core, seat, own, far, weights, share):
    features = weights[0].shape[2]
    shape = jax.ShapeDtypeStruct((3, share, features), BF16)
    return call(
        last_kernel,
        (shape, shape),
        (core, seat, own, far, *weights),
        scratch=[pltpu.VMEM(weights[0].shape[1:], BF16)],
        smem=2,
    )


def project_kernel(q_ref, wg_ref, wu_ref, wd_ref, wo_ref, out_ref, rows_ref):
    @pl.when(pl.program_id(0) == 0)
    def _():
        q = q_ref[...]
        x = nn(q, wg_ref[0])
        u = nn(q, wu_ref[0])
        act = (jax.nn.silu(x) * u).astype(BF16)
        raw = nn(act, wd_ref[0])
        factor = lax.rsqrt(jnp.mean(raw * raw, axis=-1, keepdims=True) + 1e-6)
        rows_ref[...] = (raw * factor).astype(BF16)

    out_ref[0] = nn(rows_ref[...], wo_ref[...]).astype(BF16)


def project(q, weights, w_out, parts):
    rows, features = q.shape
    columns = w_out.shape[1] // parts
    whole = pl.BlockSpec((1, features, features), lambda i: (0, 0, 0))
    return pl.pallas_call(
        project_kernel,
        grid=(parts,),
        out_shape=jax.ShapeDtypeStruct((parts, rows, columns), BF16),
        in_specs=[
            pl.BlockSpec((rows, features), lambda i: (0, 0)),
            whole,
            whole,
            whole,
            pl.BlockSpec((features, columns), lambda i: (0, i)),
        ],
        out_specs=pl.BlockSpec((1, rows, columns), lambda i: (i, 0, 0)),
        scratch_shapes=[pltpu.VMEM((rows, features), BF16)],
        compiler_params=pltpu.CompilerParams(dimension_semantics=("arbitrary",)),
    )(q, *weights, w_out)


def attend_kernel(position_ref, q_ref, k_ref, v_ref, kp_ref, vp_ref, out_ref):
    rows = q_ref.shape[0]
    has_prior = position_ref[0] > 0
    row = lax.broadcasted_iota(jnp.int32, (rows, rows), 0)
    column = lax.broadcasted_iota(jnp.int32, (rows, rows), 1)
    here = column <= row
    for h in range(q_ref.shape[1] // AD):
        cols = slice(h * AD, (h + 1) * AD)
        q = q_ref[:, cols]
        now = nt(q, k_ref[:, cols])
        before = nt(q, kp_ref[:, cols])
        before = jnp.where(has_prior, before * AD**-0.5, -1e30)
        scores = jnp.where(here, now * AD**-0.5, before)
        e = jnp.exp(scores - jnp.max(scores, axis=-1, keepdims=True))
        probs = e / jnp.sum(e, axis=-1, keepdims=True)
        probs_now = jnp.where(here, probs, 0.0).astype(BF16)
        probs_before = jnp.where(here, 0.0, probs).astype(BF16)
        out_ref[:, cols] = nn(probs_now, v_ref[:, cols]) + nn(probs_before, vp_ref[:, cols])


def attend(position, q, k, v, k_prior, v_prior):
    return call(
        attend_kernel, jax.ShapeDtypeStruct(q.shape, F32), (position, q, k, v, k_prior, v_prior), smem=1
    )


def swap(x, axis):
    return lax.ppermute(x, axis, [(0, 1), (1, 0)])


def block_sum(own, far):
    half = (own.astype(F32) + swap(far, "core").astype(F32)).astype(BF16)
    arrived = lax.all_to_all(half, CHIPS, 0, 0, tiled=True)
    return arrived.astype(F32).sum(axis=0).astype(BF16)


def from_every_chip(share):
    copies = jnp.broadcast_to(share, (lax.axis_size(CHIPS), *share.shape))
    own = lax.all_to_all(copies, CHIPS, 0, 0, tiled=True)
    return own, swap(own, "core")


def on_device(fast_q, fast_k, fast_v, rates, w_gate, w_up, w_down, w_out, att_q, att_k, att_v):
    chips = lax.axis_size(CHIPS)
    heads = lax.axis_size(HEAD)
    core = lax.axis_index("core").astype(jnp.int32).reshape(1)
    seat = lax.axis_index(SEQ[1:]).astype(jnp.int32).reshape(1)
    span = lax.axis_index("span")
    position = lax.axis_index(SEQ).astype(jnp.int32).reshape(1)
    seats = lax.axis_size(SEQ)
    rate = rates.T
    weights = (w_gate, w_up, w_down)

    route = [(i, i + 1) for i in range(seats - 1)]
    k_prior = lax.ppermute(att_k, SEQ, route)
    v_prior = lax.ppermute(att_v, SEQ, route)

    share = block_sum(*gradients(core, fast_k, fast_v, rate, weights, chips))
    share = lax.ppermute(share, "span", [(0, 1)])
    weights = update(core, *from_every_chip(share), weights)

    share = block_sum(*gradients(core, fast_k, fast_v, rate, weights, chips))
    parts = project(fast_q, weights, w_out, heads)
    parts = lax.all_to_all(parts, HEAD, 0, 0, tiled=True)
    mine, peer = last_update(
        core, seat, *from_every_chip(share), weights, w_gate.shape[1] // seats
    )
    given = lax.ppermute(peer, "span", [(1, 0)])
    final = jnp.where(span == 1, mine, given)[:, None]

    attended = attend(position, att_q, att_k, att_v, k_prior, v_prior)
    mixed = (attended + parts.astype(F32).sum(axis=0)).astype(BF16)
    return mixed, final


def solution(mesh):
    split = Mesh(mesh.devices.reshape(2, 2, 4, 2, 2, 4), (*SEQ, *HEAD))
    in_specs = (
        P(SEQ, HEAD),
        P(SEQ, HEAD),
        P(SEQ, HEAD),
        P(HEAD, SEQ),
        P(HEAD, None, None),
        P(HEAD, None, None),
        P(HEAD, None, None),
        P(HEAD, None),
        P(SEQ, HEAD),
        P(SEQ, HEAD),
        P(SEQ, HEAD),
    )
    out_specs = (P(SEQ, HEAD), P(None, HEAD, SEQ, None))
    return jax.shard_map(on_device, mesh=split, in_specs=in_specs, out_specs=out_specs, check_vma=False)
```

```python
import jax
import jax.numpy as jnp
from jax import lax
from jax.experimental import pallas as pl
from jax.experimental.pallas import tpu as pltpu
from jax.sharding import Mesh
from jax.sharding import PartitionSpec as P

AD = 128
NS_STEPS = 2
NEWTON_COEFFS = (3.4445, -4.775, 2.0315)
SEQ = ("span", "row", "y", "core")
CHIPS = ("row", "y")
HEAD = ("head_0", "head_1")
F32 = jnp.float32
BF16 = jnp.bfloat16


VMEM = pl.BlockSpec(memory_space=pltpu.VMEM)
SMEM = pl.BlockSpec(memory_space=pltpu.SMEM)
ANY = pl.BlockSpec(memory_space=pl.ANY)


def nn(a, b):
    return lax.dot_general(a, b, (((1,), (0,)), ((), ())), preferred_element_type=F32)


def nt(a, b):
    return lax.dot_general(a, b, (((1,), (1,)), ((), ())), preferred_element_type=F32)


def tn(a, b):
    return lax.dot_general(a, b, (((0,), (0,)), ((), ())), preferred_element_type=F32)


def call(kernel, outs, args, scratch=(), smem=0):
    return pl.pallas_call(
        kernel,
        out_shape=outs,
        in_specs=[SMEM] * smem + [VMEM] * (len(args) - smem),
        out_specs=jax.tree.map(lambda _: VMEM, outs),
        scratch_shapes=scratch,
    )(*args)


def start(source, target, sem):
    copy = pltpu.make_async_copy(source, target, sem)
    copy.start()
    return copy


def split_gradients(core, k, v, rate, weights, own_ref, far_ref, own_out, far_out, sem):
    weighted = (rate * v.astype(F32)).astype(BF16)
    x = nn(k, weights[0])
    u = nn(k, weights[1])
    sig = jax.nn.sigmoid(x)
    silu = x * sig
    neg_act = (-(silu * u)).astype(BF16)
    copies = []

    def emit(m, left, right):
        _, blocks, step, _ = own_ref.shape
        half = blocks * step
        for h in range(2):
            g = tn(left[:, h * half : (h + 1) * half], right).astype(BF16).reshape(own_ref.shape[1:])

            @pl.when(core == h)
            def _():
                own_ref[m] = g

            @pl.when(core != h)
            def _():
                far_ref[m] = g

        copies.append(start(own_ref.at[m], own_out.at[:, m], sem.at[m]))
        copies.append(start(far_ref.at[m], far_out.at[:, m], sem.at[3 + m]))

    emit(2, neg_act, weighted)
    back = -nt(weighted, weights[2])
    emit(1, k, (back * silu).astype(BF16))
    emit(0, k, (back * u * (sig * (1.0 + x * (1.0 - sig)))).astype(BF16))
    return copies


def column(row):
    size = row.shape[1]
    eye = lax.broadcasted_iota(jnp.int32, (size, size), 0) == lax.broadcasted_iota(
        jnp.int32, (size, size), 1
    )
    return jnp.sum(jnp.where(eye, row, 0.0), axis=1, keepdims=True)


def gradients_kernel(
    core_ref, rate_ref, k_in, v_in, wg_in, wu_in, wd_in, own_out, far_out,
    k_ref, v_ref, w_ref, own_ref, far_ref, sem, out_sem,
):
    loads = [
        start(source, target, sem.at[i])
        for i, (source, target) in enumerate(
            (
                (k_in, k_ref),
                (wg_in.at[0], w_ref.at[0]),
                (wu_in.at[0], w_ref.at[1]),
                (v_in, v_ref),
                (wd_in.at[0], w_ref.at[2]),
            )
        )
    ]
    rate = column(rate_ref[...])
    for copy in loads:
        copy.wait()
    weights = [w_ref[m] for m in range(3)]
    for copy in split_gradients(
        core_ref[0], k_ref[...], v_ref[...], rate, weights, own_ref, far_ref, own_out, far_out, out_sem
    ):
        copy.wait()


def split_shape(features, blocks):
    return (blocks, 3, features // 2 // blocks, features)


def split_scratch(features, blocks):
    return [pltpu.VMEM((3, blocks, features // 2 // blocks, features), BF16)] * 2


def gradients(core, k, v, rate, weights, blocks):
    rows, features = k.shape
    shape = jax.ShapeDtypeStruct(split_shape(features, blocks), BF16)
    return pl.pallas_call(
        gradients_kernel,
        out_shape=(shape, shape),
        in_specs=[SMEM, VMEM] + [ANY] * 5,
        out_specs=(ANY, ANY),
        scratch_shapes=[
            pltpu.VMEM((rows, features), BF16),
            pltpu.VMEM((rows, features), BF16),
            pltpu.VMEM((3, features, features), BF16),
            *split_scratch(features, blocks),
            pltpu.SemaphoreType.DMA((5,)),
            pltpu.SemaphoreType.DMA((6,)),
        ],
    )(core, rate, k, v, *weights)


def orthogonal(gradients):
    first, second, third = NEWTON_COEFFS
    xs = []
    for load in gradients:
        wide = load().astype(F32)
        xs.append((wide * lax.rsqrt(jnp.sum(wide * wide) + 1e-6)).astype(BF16))
    for _ in range(NS_STEPS):
        grams = [nt(x, x).astype(BF16) for x in xs]
        polys = [(second * g.astype(F32) + third * nn(g, g)).astype(BF16) for g in grams]
        xs = [(first * x.astype(F32) + nn(p, x)).astype(BF16) for p, x in zip(polys, xs)]
    return xs


def moved_weight(w, x):
    w = w.astype(F32)
    moved = w - x.astype(F32)
    target = jnp.sqrt(jnp.sum(w * w, axis=0, keepdims=True) + 1e-6)
    current = jnp.sqrt(jnp.sum(moved * moved, axis=0, keepdims=True) + 1e-6)
    return (moved * (target / current)).astype(BF16)


def gathered(core, own_in, far_in, g_ref, sem):
    loads = []

    def wanted(m, pair):
        def load():
            for copy in pair:
                copy.wait()
            return g_ref[m].reshape(g_ref.shape[4], g_ref.shape[4])

        return load

    for m in range(3):
        pair = (
            start(own_in.at[:, m], g_ref.at[m, core], sem.at[m]),
            start(far_in.at[:, m], g_ref.at[m, 1 - core], sem.at[3 + m]),
        )
        loads.append(wanted(m, pair))
    return loads


def update_kernel(
    core_ref, rate_ref, own_in, far_in, wg_in, wu_in, wd_in, k_in, v_in,
    wg_out, wu_out, wd_out, own_out, far_out,
    g_ref, w_ref, k_ref, v_ref, own_ref, far_ref, sem, g_sem, w_sem, out_sem,
):
    core = core_ref[0]
    loads = gathered(core, own_in, far_in, g_ref, g_sem)
    others = [start(w.at[0], w_ref.at[m], sem.at[m]) for m, w in enumerate((wg_in, wu_in, wd_in))]
    others += [start(k_in, k_ref, sem.at[3]), start(v_in, v_ref, sem.at[4])]
    rate = column(rate_ref[...])
    xs = orthogonal(loads)
    for copy in others:
        copy.wait()
    weights = [moved_weight(w_ref[m], x) for m, x in enumerate(xs)]
    copies = []
    for m, (w, out) in enumerate(zip(weights, (wg_out, wu_out, wd_out))):
        w_ref[m] = w
        copies.append(start(w_ref.at[m], out.at[0], w_sem.at[m]))
    copies += split_gradients(
        core, k_ref[...], v_ref[...], rate, weights, own_ref, far_ref, own_out, far_out, out_sem
    )
    for copy in copies:
        copy.wait()


def update(core, rate, own, far, weights, k, v):
    rows, features = k.shape
    blocks, _, step, _ = own.shape
    weight = jax.ShapeDtypeStruct(weights[0].shape, BF16)
    split = jax.ShapeDtypeStruct(own.shape, BF16)
    out = pl.pallas_call(
        update_kernel,
        out_shape=(weight,) * 3 + (split,) * 2,
        in_specs=[SMEM, VMEM] + [ANY] * 7,
        out_specs=(ANY,) * 5,
        scratch_shapes=[
            pltpu.VMEM((3, 2, blocks, step, features), BF16),
            pltpu.VMEM((3, features, features), BF16),
            pltpu.VMEM((rows, features), BF16),
            pltpu.VMEM((rows, features), BF16),
            *split_scratch(features, blocks),
            pltpu.SemaphoreType.DMA((5,)),
            pltpu.SemaphoreType.DMA((6,)),
            pltpu.SemaphoreType.DMA((3,)),
            pltpu.SemaphoreType.DMA((6,)),
        ],
    )(core, rate, own, far, *weights, k, v)
    return out[:3], out[3], out[4]


def last_kernel(
    core_ref, seat_ref, own_in, far_in, wg_in, wu_in, wd_in, mine_ref, peer_ref, g_ref, w_ref, sem, g_sem
):
    seat = seat_ref[0]
    loads = gathered(core_ref[0], own_in, far_in, g_ref, g_sem)
    others = [start(w.at[0], w_ref.at[m], sem.at[m]) for m, w in enumerate((wg_in, wu_in, wd_in))]
    share = mine_ref.shape[1]
    half = w_ref.shape[1] // 2
    xs = orthogonal(loads)
    for copy in others:
        copy.wait()
    for m, x in enumerate(xs):
        w_ref[m] = moved_weight(w_ref[m], x)
        peer_ref[m] = w_ref[m, pl.ds(pl.multiple_of(seat * share, share), share), :]
        mine_ref[m] = w_ref[m, pl.ds(pl.multiple_of(half + seat * share, share), share), :]


def last_update(core, seat, own, far, weights, share):
    blocks, _, step, features = own.shape
    shape = jax.ShapeDtypeStruct((3, share, features), BF16)
    return pl.pallas_call(
        last_kernel,
        out_shape=(shape, shape),
        in_specs=[SMEM, SMEM] + [ANY] * 5,
        out_specs=(VMEM, VMEM),
        scratch_shapes=[
            pltpu.VMEM((3, 2, blocks, step, features), BF16),
            pltpu.VMEM((3, features, features), BF16),
            pltpu.SemaphoreType.DMA((3,)),
            pltpu.SemaphoreType.DMA((6,)),
        ],
    )(core, seat, own, far, *weights)


def blocks_of(wo_in, blocks_ref, wo_ref, sem):
    columns = wo_ref.shape[2]
    return [
        start(
            wo_in.at[:, pl.ds(pl.multiple_of(blocks_ref[i] * columns, 128), columns)], wo_ref.at[i], sem.at[i]
        )
        for i in range(4)
    ]


def products(rows, loads, wo_ref, part_ref, a_out, b_out, sem):
    copies = []
    for i in range(4):
        loads[i].wait()
        part_ref[i] = nn(rows, wo_ref[i]).astype(BF16)
        copies.append(start(part_ref.at[i], (a_out, b_out)[i // 2].at[i % 2], sem.at[i]))
    for copy in copies:
        copy.wait()


def first_products_kernel(
    blocks_ref, q_in, wg_in, wu_in, wd_in, wo_in, a_out, b_out, rows_out,
    q_ref, w_ref, wo_ref, rows_ref, part_ref, sem, wo_sem, out_sem,
):
    inputs = [start(q_in, q_ref, sem.at[3])]
    inputs += [start(w.at[0], w_ref.at[m], sem.at[m]) for m, w in enumerate((wg_in, wu_in, wd_in))]
    loads = blocks_of(wo_in, blocks_ref, wo_ref, wo_sem)
    for copy in inputs:
        copy.wait()
    q = q_ref[...]
    x = nn(q, w_ref[0])
    act = (jax.nn.silu(x) * nn(q, w_ref[1])).astype(BF16)
    raw = nn(act, w_ref[2])
    rows = (raw * lax.rsqrt(jnp.mean(raw * raw, axis=-1, keepdims=True) + 1e-6)).astype(BF16)
    rows_ref[...] = rows
    kept = start(rows_ref, rows_out, sem.at[4])
    products(rows, loads, wo_ref, part_ref, a_out, b_out, out_sem)
    kept.wait()


def later_products_kernel(
    blocks_ref, rows_in, wo_in, a_out, b_out, wo_ref, rows_ref, part_ref, sem, wo_sem, out_sem
):
    kept = start(rows_in, rows_ref, sem)
    loads = blocks_of(wo_in, blocks_ref, wo_ref, wo_sem)
    kept.wait()
    products(rows_ref[...], loads, wo_ref, part_ref, a_out, b_out, out_sem)


def first_products(blocks, q, weights, w_out, heads):
    rows, features = q.shape
    columns = w_out.shape[1] // heads
    pair = jax.ShapeDtypeStruct((2, rows, columns), BF16)
    return pl.pallas_call(
        first_products_kernel,
        out_shape=(pair, pair, jax.ShapeDtypeStruct((rows, features), BF16)),
        in_specs=[SMEM] + [ANY] * 5,
        out_specs=(ANY,) * 3,
        scratch_shapes=[
            pltpu.VMEM((rows, features), BF16),
            pltpu.VMEM((3, features, features), BF16),
            pltpu.VMEM((4, features, columns), BF16),
            pltpu.VMEM((rows, features), BF16),
            pltpu.VMEM((4, rows, columns), BF16),
            pltpu.SemaphoreType.DMA((5,)),
            pltpu.SemaphoreType.DMA((4,)),
            pltpu.SemaphoreType.DMA((4,)),
        ],
    )(blocks, q, *weights, w_out)


def later_products(blocks, rows, w_out, heads):
    features = rows.shape[1]
    columns = w_out.shape[1] // heads
    pair = jax.ShapeDtypeStruct((2, rows.shape[0], columns), BF16)
    return pl.pallas_call(
        later_products_kernel,
        out_shape=(pair, pair),
        in_specs=[SMEM] + [ANY] * 2,
        out_specs=(ANY,) * 2,
        scratch_shapes=[
            pltpu.VMEM((4, features, columns), BF16),
            pltpu.VMEM(rows.shape, BF16),
            pltpu.VMEM((4, rows.shape[0], columns), BF16),
            pltpu.SemaphoreType.DMA,
            pltpu.SemaphoreType.DMA((4,)),
            pltpu.SemaphoreType.DMA((4,)),
        ],
    )(blocks, rows, w_out)


def halve_kernel(a_ref, ar_ref, b_ref, br_ref, a_keep, a_send, b_keep, b_send):
    for kept, come, keep, send in ((a_ref, ar_ref, a_keep, a_send), (b_ref, br_ref, b_keep, b_send)):
        keep[...] = (kept[0].astype(F32) + come[0].astype(F32)).astype(BF16)
        send[...] = (kept[1].astype(F32) + come[1].astype(F32)).astype(BF16)


def halve(a, a_come, b, b_come):
    shape = jax.ShapeDtypeStruct(a.shape[1:], BF16)
    return call(halve_kernel, (shape,) * 4, (a, a_come, b, b_come))


def choose_kernel(far_ref, a_ref, ar_ref, b_ref, br_ref, keep_ref, send_ref):
    a = (a_ref[...].astype(F32) + ar_ref[...].astype(F32)).astype(BF16)
    b = (b_ref[...].astype(F32) + br_ref[...].astype(F32)).astype(BF16)
    second = far_ref[0] == 1
    keep_ref[...] = jnp.where(second, b, a)
    send_ref[...] = jnp.where(second, a, b)


def choose(far, a, a_come, b, b_come):
    shape = jax.ShapeDtypeStruct(a.shape, BF16)
    return call(choose_kernel, (shape, shape), (far, a, a_come, b, b_come), smem=1)


def attend_kernel(position_ref, q_ref, k_ref, v_ref, kp_ref, vp_ref, out_ref):
    rows = q_ref.shape[0]
    has_prior = position_ref[0] > 0
    row = lax.broadcasted_iota(jnp.int32, (rows, rows), 0)
    column = lax.broadcasted_iota(jnp.int32, (rows, rows), 1)
    here = column <= row
    for h in range(q_ref.shape[1] // AD):
        cols = slice(h * AD, (h + 1) * AD)
        q = q_ref[:, cols]
        now = nt(q, k_ref[:, cols])
        before = nt(q, kp_ref[:, cols])
        before = jnp.where(has_prior, before * AD**-0.5, -1e30)
        scores = jnp.where(here, now * AD**-0.5, before)
        e = jnp.exp(scores - jnp.max(scores, axis=-1, keepdims=True))
        probs = e / jnp.sum(e, axis=-1, keepdims=True)
        probs_now = jnp.where(here, probs, 0.0).astype(BF16)
        probs_before = jnp.where(here, 0.0, probs).astype(BF16)
        out_ref[:, cols] = nn(probs_now, v_ref[:, cols]) + nn(probs_before, vp_ref[:, cols])


def attend(position, q, k, v, k_prior, v_prior):
    return call(
        attend_kernel, jax.ShapeDtypeStruct(q.shape, F32), (position, q, k, v, k_prior, v_prior), smem=1
    )


def swap(x, axis):
    return lax.ppermute(x, axis, [(0, 1), (1, 0)])


def half_sum(own, come):
    return (own.astype(F32) + come.astype(F32)).astype(BF16)


def block_sum(half):
    arrived = lax.all_to_all(half, CHIPS, 0, 0, tiled=True)
    return arrived.astype(F32).sum(axis=0).astype(BF16)


def from_every_chip(share):
    copies = jnp.broadcast_to(share, (lax.axis_size(CHIPS), *share.shape))
    return lax.all_to_all(copies, CHIPS, 0, 0, tiled=True)


def near(x):
    return pltpu.with_memory_space_constraint(x, pltpu.VMEM)


def together(*arrays):
    return lax.optimization_barrier(arrays)


def flip(x, mask):
    devices = range(lax.axis_size(HEAD[1]))
    return lax.ppermute(x, HEAD[1], [(i, i ^ mask) for i in devices])


def on_device(fast_q, fast_k, fast_v, rates, w_gate, w_up, w_down, w_out, att_q, att_k, att_v):
    chips = lax.axis_size(CHIPS)
    heads = lax.axis_size(HEAD)
    core = lax.axis_index("core").astype(jnp.int32).reshape(1)
    seat = lax.axis_index(SEQ[1:]).astype(jnp.int32).reshape(1)
    span = lax.axis_index("span")
    position = lax.axis_index(SEQ).astype(jnp.int32).reshape(1)
    seats = lax.axis_size(SEQ)
    far = lax.axis_index(HEAD[0]).astype(jnp.int32).reshape(1)
    x = lax.axis_index(HEAD[1]).astype(jnp.int32)
    line = lax.axis_size(HEAD[1])
    weights = (w_gate, w_up, w_down)

    route = [(i, i + 1) for i in range(seats - 1)]
    k_prior = lax.ppermute(att_k, SEQ, route)
    v_prior = lax.ppermute(att_v, SEQ, route)

    own, away = gradients(core, fast_k, fast_v, rates, weights, chips)
    share = block_sum(half_sum(own, swap(away, "core")))
    given = lax.ppermute(share, "span", [(0, 1)])
    k_prior, v_prior, share = together(k_prior, v_prior, share)
    attended = attend(position, att_q, att_k, att_v, near(k_prior), near(v_prior))
    given, attended = together(given, attended)
    own = from_every_chip(given)
    weights, own, away = update(core, rates, near(own), near(swap(own, "core")), weights, fast_k, fast_v)

    sent = jnp.stack([x ^ 1, x ^ 2, line + (x ^ 3), line + (x ^ 2)])
    held = jnp.stack([x, x ^ 3, line + x, line + (x ^ 1)])
    come = swap(away, "core")
    a_sent, b_sent, rows = first_products(sent, fast_q, weights, w_out, heads)
    come, a_sent, b_sent, rows = together(come, a_sent, b_sent, rows)
    a_come = flip(a_sent, 1)
    b_come = flip(b_sent, 3)
    a_held, b_held = later_products(held, rows, w_out, heads)
    share = block_sum(half_sum(own, come))
    share, a_held, b_held = together(share, a_held, b_held)
    a_held, a_sent, b_held, b_sent = halve(a_held, near(a_come), b_held, near(b_come))
    a_come = flip(a_sent, 3)
    b_come = flip(b_sent, 1)
    own = from_every_chip(share)
    own, a_sent, b_sent = together(own, a_sent, b_sent)
    away = swap(own, "core")
    held, sent = choose(far, a_held, near(a_come), b_held, near(b_come))
    come = swap(sent, HEAD[0])

    mine, peer = last_update(core, seat, near(own), near(away), weights, w_gate.shape[1] // seats)
    given = lax.ppermute(peer, "span", [(1, 0)])
    final = jnp.where(span == 1, mine, given)[:, None]
    mixed = (attended + held.astype(F32) + come.astype(F32)).astype(BF16)
    return mixed, final


def solution(mesh):
    split = Mesh(mesh.devices.reshape(2, 2, 4, 2, 2, 4), (*SEQ, *HEAD))
    in_specs = (
        P(SEQ, HEAD),
        P(SEQ, HEAD),
        P(SEQ, HEAD),
        P(HEAD, SEQ),
        P(HEAD, None, None),
        P(HEAD, None, None),
        P(HEAD, None, None),
        P(HEAD, None),
        P(SEQ, HEAD),
        P(SEQ, HEAD),
        P(SEQ, HEAD),
    )
    out_specs = (P(SEQ, HEAD), P(None, HEAD, SEQ, None))
    return jax.shard_map(on_device, mesh=split, in_specs=in_specs, out_specs=out_specs, check_vma=False)
```

```python
import functools

import jax
import jax.numpy as jnp
from jax import lax
from jax.experimental import pallas as pl
from jax.experimental.pallas import tpu as pltpu
from jax.sharding import Mesh
from jax.sharding import PartitionSpec as P

AD = 128
NS_STEPS = 2
NEWTON_COEFFS = (3.4445, -4.775, 2.0315)
SEQ = ("span", "row", "y", "core")
CHIPS = ("row", "y")
HEAD = ("head_0", "head_1")
F32 = jnp.float32
BF16 = jnp.bfloat16


VMEM = pl.BlockSpec(memory_space=pltpu.VMEM)
SMEM = pl.BlockSpec(memory_space=pltpu.SMEM)
HBM = pl.BlockSpec(memory_space=pltpu.HBM)
ROOM = pltpu.CompilerParams(vmem_limit_bytes=20 << 20)


def nn(a, b):
    return lax.dot_general(a, b, (((1,), (0,)), ((), ())), preferred_element_type=F32)


def nt(a, b):
    return lax.dot_general(a, b, (((1,), (1,)), ((), ())), preferred_element_type=F32)


def tn(a, b):
    return lax.dot_general(a, b, (((0,), (0,)), ((), ())), preferred_element_type=F32)


def call(kernel, outs, args, scratch=(), smem=0):
    return pl.pallas_call(
        kernel,
        out_shape=outs,
        in_specs=[SMEM] * smem + [VMEM] * (len(args) - smem),
        out_specs=jax.tree.map(lambda _: VMEM, outs),
        scratch_shapes=scratch,
        compiler_params=ROOM,
    )(*args)


def start(source, target, sem):
    copy = pltpu.make_async_copy(source, target, sem)
    copy.start()
    return copy


def split_gradients(core, k, v, rate, weights, own_ref, far_ref):
    weighted = (rate * v.astype(F32)).astype(BF16)
    x = nn(k, weights[0])
    u = nn(k, weights[1])
    sig = jax.nn.sigmoid(x)
    silu = x * sig
    neg_act = (-(silu * u)).astype(BF16)

    def emit(m, left, right):
        blocks, _, step, features = own_ref.shape
        half = blocks * step
        for h in range(2):
            g = tn(left[:, h * half : (h + 1) * half], right).astype(BF16).reshape(blocks, step, features)

            @pl.when(core == h)
            def _():
                own_ref[:, m] = g

            @pl.when(core != h)
            def _():
                far_ref[:, m] = g

    emit(2, neg_act, weighted)
    back = -nt(weighted, weights[2])
    emit(1, k, (back * silu).astype(BF16))
    emit(0, k, (back * u * (sig * (1.0 + x * (1.0 - sig)))).astype(BF16))


def column(row):
    size = row.shape[1]
    eye = lax.broadcasted_iota(jnp.int32, (size, size), 0) == lax.broadcasted_iota(
        jnp.int32, (size, size), 1
    )
    return jnp.sum(jnp.where(eye, row, 0.0), axis=1, keepdims=True)


def gradients_kernel(
    core_ref, rate_in, k_in, v_in, wg_in, wu_in, wd_in, own_ref, far_ref, rate_ref, k_ref, v_ref, w_ref, sem
):
    loads = [
        start(source, target, sem.at[i])
        for i, (source, target) in enumerate(
            (
                (k_in, k_ref),
                (wg_in.at[0], w_ref.at[0]),
                (wu_in.at[0], w_ref.at[1]),
                (v_in, v_ref),
                (wd_in.at[0], w_ref.at[2]),
                (rate_in, rate_ref),
            )
        )
    ]
    for copy in loads:
        copy.wait()
    rate = column(rate_ref[...])
    weights = [w_ref[m] for m in range(3)]
    split_gradients(core_ref[0], k_ref[...], v_ref[...], rate, weights, own_ref, far_ref)


def split_shape(features, blocks):
    return (blocks, 3, features // 2 // blocks, features)


def gradients(core, k, v, rate, weights, blocks):
    rows, features = k.shape
    shape = pltpu.VMEM(split_shape(features, blocks), BF16)
    return pl.pallas_call(
        gradients_kernel,
        out_shape=(shape, shape),
        in_specs=[SMEM] + [HBM] * 6,
        out_specs=(VMEM, VMEM),
        scratch_shapes=[
            pltpu.VMEM(rate.shape, F32),
            pltpu.VMEM((rows, features), BF16),
            pltpu.VMEM((rows, features), BF16),
            pltpu.VMEM((3, features, features), BF16),
            pltpu.SemaphoreType.DMA((6,)),
        ],
        compiler_params=ROOM,
    )(core, rate, k, v, *weights)


def orthogonal(gradients):
    first, second, third = NEWTON_COEFFS
    xs = []
    for load in gradients:
        wide = load().astype(F32)
        xs.append((wide * lax.rsqrt(jnp.sum(wide * wide) + 1e-6)).astype(BF16))
    for _ in range(NS_STEPS):
        grams = [nt(x, x).astype(BF16) for x in xs]
        polys = [(second * g.astype(F32) + third * nn(g, g)).astype(BF16) for g in grams]
        xs = [(first * x.astype(F32) + nn(p, x)).astype(BF16) for p, x in zip(polys, xs)]
    return xs


def moved_weight(w, x):
    w = w.astype(F32)
    moved = w - x.astype(F32)
    target = jnp.sqrt(jnp.sum(w * w, axis=0, keepdims=True) + 1e-6)
    current = jnp.sqrt(jnp.sum(moved * moved, axis=0, keepdims=True) + 1e-6)
    return (moved * (target / current)).astype(BF16)


def gathered(core, own_in, far_in, g_ref, sem):
    loads = []

    def wanted(m, pair):
        def load():
            for copy in pair:
                copy.wait()
            return g_ref[m].reshape(g_ref.shape[4], g_ref.shape[4])

        return load

    for m in range(3):
        pair = (
            start(own_in.at[:, m], g_ref.at[m, core], sem.at[m]),
            start(far_in.at[:, m], g_ref.at[m, 1 - core], sem.at[3 + m]),
        )
        loads.append(wanted(m, pair))
    return loads


def update_kernel(
    core_ref, rate_in, own_in, far_in, wg_in, wu_in, wd_in, k_in, v_in,
    wg_ref, wu_ref, wd_ref, own_ref, far_ref, g_ref, rate_ref, w_ref, k_ref, v_ref, sem, g_sem,
):
    core = core_ref[0]
    loads = gathered(core, own_in, far_in, g_ref, g_sem)
    others = [start(w.at[0], w_ref.at[m], sem.at[m]) for m, w in enumerate((wg_in, wu_in, wd_in))]
    others += [start(k_in, k_ref, sem.at[3]), start(v_in, v_ref, sem.at[4]), start(rate_in, rate_ref, sem.at[5])]
    xs = orthogonal(loads)
    for copy in others:
        copy.wait()
    rate = column(rate_ref[...])
    weights = [moved_weight(w_ref[m], x) for m, x in enumerate(xs)]
    for w, out in zip(weights, (wg_ref, wu_ref, wd_ref)):
        out[0] = w
    split_gradients(core, k_ref[...], v_ref[...], rate, weights, own_ref, far_ref)


def update(core, rate, own, far, weights, k, v):
    rows, features = k.shape
    blocks, _, step, _ = own.shape
    weight = pltpu.VMEM(weights[0].shape, BF16)
    split = pltpu.VMEM(own.shape, BF16)
    out = pl.pallas_call(
        update_kernel,
        compiler_params=ROOM,
        out_shape=(weight,) * 3 + (split,) * 2,
        in_specs=[SMEM, HBM, VMEM, VMEM] + [HBM] * 5,
        out_specs=(VMEM,) * 5,
        scratch_shapes=[
            pltpu.VMEM((3, 2, blocks, step, features), BF16),
            pltpu.VMEM(rate.shape, F32),
            pltpu.VMEM((3, features, features), BF16),
            pltpu.VMEM((rows, features), BF16),
            pltpu.VMEM((rows, features), BF16),
            pltpu.SemaphoreType.DMA((6,)),
            pltpu.SemaphoreType.DMA((6,)),
        ],
    )(core, rate, own, far, *weights, k, v)
    return out[:3], out[3], out[4]


def last_kernel(
    core_ref, seat_ref, own_in, far_in, wg_ref, wu_ref, wd_ref, mine_ref, peer_ref, g_ref, w_ref, g_sem
):
    seat = seat_ref[0]
    loads = gathered(core_ref[0], own_in, far_in, g_ref, g_sem)
    share = mine_ref.shape[1]
    half = w_ref.shape[1] // 2
    for m, (old_ref, x) in enumerate(zip((wg_ref, wu_ref, wd_ref), orthogonal(loads))):
        w_ref[m] = moved_weight(old_ref[0], x)
        peer_ref[m] = w_ref[m, pl.ds(pl.multiple_of(seat * share, share), share), :]
        mine_ref[m] = w_ref[m, pl.ds(pl.multiple_of(half + seat * share, share), share), :]


def last_update(core, seat, own, far, weights, share):
    blocks, _, step, features = own.shape
    shape = jax.ShapeDtypeStruct((3, share, features), BF16)
    return pl.pallas_call(
        last_kernel,
        out_shape=(shape, shape),
        in_specs=[SMEM, SMEM] + [VMEM] * 5,
        out_specs=(VMEM, VMEM),
        scratch_shapes=[
            pltpu.VMEM((3, 2, blocks, step, features), BF16),
            pltpu.VMEM((3, features, features), BF16),
            pltpu.SemaphoreType.DMA((6,)),
        ],
        compiler_params=ROOM,
    )(core, seat, own, far, *weights)


def blocks_of(place, wo_in, wo_ref, sem):
    x_ref, masks, line = place
    columns = wo_ref.shape[2]
    loads = []
    for i, (group, mask) in enumerate(masks):
        block = line * group + jnp.bitwise_xor(x_ref[0], mask)
        columns_of = pl.ds(pl.multiple_of(block * columns, 128), columns)
        loads.append(start(wo_in.at[:, columns_of], wo_ref.at[i], sem.at[i]))
    return loads


def products(rows, loads, wo_ref, a_ref, b_ref):
    for i in range(4):
        loads[i].wait()
        (a_ref, b_ref)[i // 2][i % 2] = nn(rows, wo_ref[i]).astype(BF16)


def first_products_kernel(
    masks, line, x_ref, q_in, wg_ref, wu_ref, wd_ref, wo_in, a_ref, b_ref, rows_ref, q_ref, wo_ref, sem, wo_sem
):
    query = start(q_in, q_ref, sem)
    loads = blocks_of((x_ref, masks, line), wo_in, wo_ref, wo_sem)
    query.wait()
    q = q_ref[...]
    x = nn(q, wg_ref[0])
    act = (jax.nn.silu(x) * nn(q, wu_ref[0])).astype(BF16)
    raw = nn(act, wd_ref[0])
    rows = (raw * lax.rsqrt(jnp.mean(raw * raw, axis=-1, keepdims=True) + 1e-6)).astype(BF16)
    rows_ref[...] = rows
    products(rows, loads, wo_ref, a_ref, b_ref)


def later_products_kernel(masks, line, x_ref, rows_ref, wo_in, a_ref, b_ref, wo_ref, wo_sem):
    loads = blocks_of((x_ref, masks, line), wo_in, wo_ref, wo_sem)
    products(rows_ref[...], loads, wo_ref, a_ref, b_ref)


def first_products(masks, line, x, q, weights, w_out, heads):
    rows, features = q.shape
    columns = w_out.shape[1] // heads
    pair = pltpu.VMEM((2, rows, columns), BF16)
    return pl.pallas_call(
        functools.partial(first_products_kernel, masks, line),
        out_shape=(pair, pair, pltpu.VMEM((rows, features), BF16)),
        in_specs=[SMEM, HBM, VMEM, VMEM, VMEM, HBM],
        out_specs=(VMEM,) * 3,
        scratch_shapes=[
            pltpu.VMEM((rows, features), BF16),
            pltpu.VMEM((4, features, columns), BF16),
            pltpu.SemaphoreType.DMA,
            pltpu.SemaphoreType.DMA((4,)),
        ],
        compiler_params=ROOM,
    )(x, q, *weights, w_out)


def later_products(masks, line, x, rows, w_out, heads):
    features = rows.shape[1]
    columns = w_out.shape[1] // heads
    pair = pltpu.VMEM((2, rows.shape[0], columns), BF16)
    return pl.pallas_call(
        functools.partial(later_products_kernel, masks, line),
        out_shape=(pair, pair),
        in_specs=[SMEM, VMEM, HBM],
        out_specs=(VMEM, VMEM),
        scratch_shapes=[pltpu.VMEM((4, features, columns), BF16), pltpu.SemaphoreType.DMA((4,))],
        compiler_params=ROOM,
    )(x, rows, w_out)


def halve_kernel(a_ref, ar_ref, b_ref, br_ref, a_keep, a_send, b_keep, b_send):
    for kept, come, keep, send in ((a_ref, ar_ref, a_keep, a_send), (b_ref, br_ref, b_keep, b_send)):
        keep[...] = (kept[0].astype(F32) + come[0].astype(F32)).astype(BF16)
        send[...] = (kept[1].astype(F32) + come[1].astype(F32)).astype(BF16)


def halve(a, a_come, b, b_come):
    shape = jax.ShapeDtypeStruct(a.shape[1:], BF16)
    return call(halve_kernel, (shape,) * 4, (a, a_come, b, b_come))


def choose_kernel(far_ref, a_ref, ar_ref, b_ref, br_ref, keep_ref, send_ref):
    a = (a_ref[...].astype(F32) + ar_ref[...].astype(F32)).astype(BF16)
    b = (b_ref[...].astype(F32) + br_ref[...].astype(F32)).astype(BF16)
    second = far_ref[0] == 1
    keep_ref[...] = jnp.where(second, b, a)
    send_ref[...] = jnp.where(second, a, b)


def choose(far, a, a_come, b, b_come):
    shape = jax.ShapeDtypeStruct(a.shape, BF16)
    return call(choose_kernel, (shape, shape), (far, a, a_come, b, b_come), smem=1)


def attend_kernel(position_ref, q_ref, k_ref, v_ref, kp_ref, vp_ref, out_ref):
    rows = q_ref.shape[0]
    has_prior = position_ref[0] > 0
    row = lax.broadcasted_iota(jnp.int32, (rows, rows), 0)
    column = lax.broadcasted_iota(jnp.int32, (rows, rows), 1)
    here = column <= row
    for h in range(q_ref.shape[1] // AD):
        cols = slice(h * AD, (h + 1) * AD)
        q = q_ref[:, cols]
        now = nt(q, k_ref[:, cols])
        before = nt(q, kp_ref[:, cols])
        before = jnp.where(has_prior, before * AD**-0.5, -1e30)
        scores = jnp.where(here, now * AD**-0.5, before)
        e = jnp.exp(scores - jnp.max(scores, axis=-1, keepdims=True))
        probs = e / jnp.sum(e, axis=-1, keepdims=True)
        probs_now = jnp.where(here, probs, 0.0).astype(BF16)
        probs_before = jnp.where(here, 0.0, probs).astype(BF16)
        out_ref[:, cols] = nn(probs_now, v_ref[:, cols]) + nn(probs_before, vp_ref[:, cols])


def attend(position, q, k, v, k_prior, v_prior):
    return call(
        attend_kernel, pltpu.VMEM(q.shape, F32), (position, q, k, v, k_prior, v_prior), smem=1
    )


def swap(x, axis):
    return lax.ppermute(x, axis, [(0, 1), (1, 0)])


def half_sum(own, come):
    return (own.astype(F32) + come.astype(F32)).astype(BF16)


def block_sum(half):
    arrived = lax.all_to_all(half, CHIPS, 0, 0, tiled=True)
    return arrived.astype(F32).sum(axis=0).astype(BF16)


def from_every_chip(share):
    copies = jnp.broadcast_to(share, (lax.axis_size(CHIPS), *share.shape))
    return lax.all_to_all(near(copies), CHIPS, 0, 0, tiled=True)


def near(x):
    return pltpu.with_memory_space_constraint(x, pltpu.VMEM)


def stored(x):
    return pltpu.with_memory_space_constraint(x, pltpu.HBM)


def together(*arrays):
    return lax.optimization_barrier(arrays)


def flip(x, mask):
    devices = range(lax.axis_size(HEAD[1]))
    return lax.ppermute(x, HEAD[1], [(i, i ^ mask) for i in devices])


def on_device(fast_q, fast_k, fast_v, rates, w_gate, w_up, w_down, w_out, att_q, att_k, att_v):
    chips = lax.axis_size(CHIPS)
    heads = lax.axis_size(HEAD)
    core = lax.axis_index("core").astype(jnp.int32).reshape(1)
    seat = lax.axis_index(SEQ[1:]).astype(jnp.int32).reshape(1)
    span = lax.axis_index("span")
    position = lax.axis_index(SEQ).astype(jnp.int32).reshape(1)
    seats = lax.axis_size(SEQ)
    far = lax.axis_index(HEAD[0]).astype(jnp.int32).reshape(1)
    x = lax.axis_index(HEAD[1]).astype(jnp.int32).reshape(1)
    line = lax.axis_size(HEAD[1])
    fast_q, fast_k, fast_v, rates, w_out = map(stored, (fast_q, fast_k, fast_v, rates, w_out))
    weights = tuple(map(stored, (w_gate, w_up, w_down)))

    route = [(i, i + 1) for i in range(seats - 1)]
    k_prior = lax.ppermute(att_k, SEQ, route)
    v_prior = lax.ppermute(att_v, SEQ, route)

    own, away = gradients(core, fast_k, fast_v, rates, weights, chips)
    share = block_sum(half_sum(own, swap(away, "core")))
    given = lax.ppermute(share, "span", [(0, 1)])
    k_prior, v_prior, share = together(k_prior, v_prior, share)
    attended = attend(position, att_q, att_k, att_v, near(k_prior), near(v_prior))
    given, attended = together(given, attended)
    own = from_every_chip(given)
    weights, own, away = update(core, rates, near(own), near(swap(own, "core")), weights, fast_k, fast_v)

    sent = ((0, 1), (0, 2), (1, 3), (1, 2))
    held = ((0, 0), (0, 3), (1, 0), (1, 1))
    come = swap(away, "core")
    a_sent, b_sent, rows = first_products(sent, line, x, fast_q, weights, w_out, heads)
    come, a_sent, b_sent, rows = together(come, a_sent, b_sent, rows)
    a_come = flip(a_sent, 1)
    b_come = flip(b_sent, 3)
    a_held, b_held = later_products(held, line, x, rows, w_out, heads)
    share = block_sum(half_sum(own, come))
    a_held, a_sent, b_held, b_sent = halve(a_held, near(a_come), b_held, near(b_come))
    a_come = flip(a_sent, 3)
    b_come = flip(b_sent, 1)
    own = from_every_chip(share)
    held, sent = choose(far, a_held, near(a_come), b_held, near(b_come))
    come = swap(sent, HEAD[0])
    away = swap(own, "core")

    mine, peer = last_update(core, seat, near(own), near(away), weights, w_gate.shape[1] // seats)
    given = lax.ppermute(peer, "span", [(1, 0)])
    final = jnp.where(span == 1, mine, given)[:, None]
    mixed = (attended + held.astype(F32) + come.astype(F32)).astype(BF16)
    return mixed, final


def solution(mesh):
    split = Mesh(mesh.devices.reshape(2, 2, 4, 2, 2, 4), (*SEQ, *HEAD))
    in_specs = (
        P(SEQ, HEAD),
        P(SEQ, HEAD),
        P(SEQ, HEAD),
        P(HEAD, SEQ),
        P(HEAD, None, None),
        P(HEAD, None, None),
        P(HEAD, None, None),
        P(HEAD, None),
        P(SEQ, HEAD),
        P(SEQ, HEAD),
        P(SEQ, HEAD),
    )
    out_specs = (P(SEQ, HEAD), P(None, HEAD, SEQ, None))
    return jax.shard_map(on_device, mesh=split, in_specs=in_specs, out_specs=out_specs, check_vma=False)
```

```python
import functools

import jax
import jax.numpy as jnp
from jax import lax
from jax.experimental import pallas as pl
from jax.experimental.pallas import tpu as pltpu
from jax.sharding import Mesh
from jax.sharding import PartitionSpec as P

AD = 128
NS_STEPS = 2
NEWTON_COEFFS = (3.4445, -4.775, 2.0315)
SEQ = ("span", "row", "y", "core")
CHIPS = ("row", "y")
HEAD = ("head_0", "head_1")
F32 = jnp.float32
BF16 = jnp.bfloat16


VMEM = pl.BlockSpec(memory_space=pltpu.VMEM)
SMEM = pl.BlockSpec(memory_space=pltpu.SMEM)
HBM = pl.BlockSpec(memory_space=pltpu.HBM)
ROOM = pltpu.CompilerParams(vmem_limit_bytes=20 << 20)


def nn(a, b):
    return lax.dot_general(a, b, (((1,), (0,)), ((), ())), preferred_element_type=F32)


def nt(a, b):
    return lax.dot_general(a, b, (((1,), (1,)), ((), ())), preferred_element_type=F32)


def tn(a, b):
    return lax.dot_general(a, b, (((0,), (0,)), ((), ())), preferred_element_type=F32)


def call(kernel, outs, args, scratch=(), smem=0):
    return pl.pallas_call(
        kernel,
        out_shape=outs,
        in_specs=[SMEM] * smem + [VMEM] * (len(args) - smem),
        out_specs=jax.tree.map(lambda _: VMEM, outs),
        scratch_shapes=scratch,
        compiler_params=ROOM,
    )(*args)


def start(source, target, sem):
    copy = pltpu.make_async_copy(source, target, sem)
    copy.start()
    return copy


def split_gradients(core, k, v, rate, weights, own_ref, far_ref):
    weighted = (rate * v.astype(F32)).astype(BF16)
    x = nn(k, weights[0])
    u = nn(k, weights[1])
    sig = jax.nn.sigmoid(x)
    silu = x * sig
    neg_act = (-(silu * u)).astype(BF16)

    def emit(m, left, right):
        blocks, _, step, features = own_ref.shape
        half = blocks * step
        for h in range(2):
            g = tn(left[:, h * half : (h + 1) * half], right).astype(BF16).reshape(blocks, step, features)

            @pl.when(core == h)
            def _():
                own_ref[:, m] = g

            @pl.when(core != h)
            def _():
                far_ref[:, m] = g

    emit(2, neg_act, weighted)
    back = -nt(weighted, weights[2])
    emit(1, k, (back * silu).astype(BF16))
    emit(0, k, (back * u * (sig * (1.0 + x * (1.0 - sig)))).astype(BF16))


def column(row):
    size = row.shape[1]
    eye = lax.broadcasted_iota(jnp.int32, (size, size), 0) == lax.broadcasted_iota(
        jnp.int32, (size, size), 1
    )
    return jnp.sum(jnp.where(eye, row, 0.0), axis=1, keepdims=True)


def gradients_kernel(
    core_ref, rate_in, k_in, v_in, wg_in, wu_in, wd_in, own_ref, far_ref, rate_ref, k_ref, v_ref, w_ref, sem
):
    loads = [
        start(source, target, sem.at[i])
        for i, (source, target) in enumerate(
            (
                (k_in, k_ref),
                (wg_in.at[0], w_ref.at[0]),
                (wu_in.at[0], w_ref.at[1]),
                (v_in, v_ref),
                (wd_in.at[0], w_ref.at[2]),
                (rate_in, rate_ref),
            )
        )
    ]
    for copy in loads:
        copy.wait()
    rate = column(rate_ref[...])
    weights = [w_ref[m] for m in range(3)]
    split_gradients(core_ref[0], k_ref[...], v_ref[...], rate, weights, own_ref, far_ref)


def split_shape(features, blocks):
    return (blocks, 3, features // 2 // blocks, features)


def gradients(core, k, v, rate, weights, blocks):
    rows, features = k.shape
    shape = pltpu.VMEM(split_shape(features, blocks), BF16)
    return pl.pallas_call(
        gradients_kernel,
        out_shape=(shape, shape),
        in_specs=[SMEM] + [HBM] * 6,
        out_specs=(VMEM, VMEM),
        scratch_shapes=[
            pltpu.VMEM(rate.shape, F32),
            pltpu.VMEM((rows, features), BF16),
            pltpu.VMEM((rows, features), BF16),
            pltpu.VMEM((3, features, features), BF16),
            pltpu.SemaphoreType.DMA((6,)),
        ],
        compiler_params=ROOM,
    )(core, rate, k, v, *weights)


def orthogonal(gradients):
    first, second, third = NEWTON_COEFFS
    xs = []
    for load in gradients:
        wide = load().astype(F32)
        xs.append((wide * lax.rsqrt(jnp.sum(wide * wide) + 1e-6)).astype(BF16))
    for _ in range(NS_STEPS):
        grams = [nt(x, x).astype(BF16) for x in xs]
        polys = [(second * g.astype(F32) + third * nn(g, g)).astype(BF16) for g in grams]
        xs = [(first * x.astype(F32) + nn(p, x)).astype(BF16) for p, x in zip(polys, xs)]
    return xs


def moved_weight(w, x):
    w = w.astype(F32)
    moved = w - x.astype(F32)
    target = jnp.sqrt(jnp.sum(w * w, axis=0, keepdims=True) + 1e-6)
    current = jnp.sqrt(jnp.sum(moved * moved, axis=0, keepdims=True) + 1e-6)
    return (moved * (target / current)).astype(BF16)


def gathered(core, own_in, far_in, g_ref, sem):
    loads = []

    def wanted(m, pair):
        def load():
            for copy in pair:
                copy.wait()
            return g_ref[m].reshape(g_ref.shape[4], g_ref.shape[4])

        return load

    for m in range(3):
        pair = (
            start(own_in.at[:, m], g_ref.at[m, core], sem.at[m]),
            start(far_in.at[:, m], g_ref.at[m, 1 - core], sem.at[3 + m]),
        )
        loads.append(wanted(m, pair))
    return loads


def update_kernel(
    core_ref, rate_in, own_in, far_in, wg_in, wu_in, wd_in, k_in, v_in,
    wg_ref, wu_ref, wd_ref, own_ref, far_ref, g_ref, rate_ref, w_ref, k_ref, v_ref, sem, g_sem,
):
    core = core_ref[0]
    loads = gathered(core, own_in, far_in, g_ref, g_sem)
    others = [start(w.at[0], w_ref.at[m], sem.at[m]) for m, w in enumerate((wg_in, wu_in, wd_in))]
    others += [start(k_in, k_ref, sem.at[3]), start(v_in, v_ref, sem.at[4]), start(rate_in, rate_ref, sem.at[5])]
    xs = orthogonal(loads)
    for copy in others:
        copy.wait()
    rate = column(rate_ref[...])
    weights = [moved_weight(w_ref[m], x) for m, x in enumerate(xs)]
    for w, out in zip(weights, (wg_ref, wu_ref, wd_ref)):
        out[0] = w
    split_gradients(core, k_ref[...], v_ref[...], rate, weights, own_ref, far_ref)


def update(core, rate, own, far, weights, k, v):
    rows, features = k.shape
    blocks, _, step, _ = own.shape
    weight = pltpu.VMEM(weights[0].shape, BF16)
    split = pltpu.VMEM(own.shape, BF16)
    out = pl.pallas_call(
        update_kernel,
        compiler_params=ROOM,
        out_shape=(weight,) * 3 + (split,) * 2,
        in_specs=[SMEM, HBM, VMEM, VMEM] + [HBM] * 5,
        out_specs=(VMEM,) * 5,
        scratch_shapes=[
            pltpu.VMEM((3, 2, blocks, step, features), BF16),
            pltpu.VMEM(rate.shape, F32),
            pltpu.VMEM((3, features, features), BF16),
            pltpu.VMEM((rows, features), BF16),
            pltpu.VMEM((rows, features), BF16),
            pltpu.SemaphoreType.DMA((6,)),
            pltpu.SemaphoreType.DMA((6,)),
        ],
    )(core, rate, own, far, *weights, k, v)
    return out[:3], out[3], out[4]


def last_kernel(
    core_ref, seat_ref, own_in, far_in, wg_ref, wu_ref, wd_ref, mine_ref, peer_ref, g_ref, w_ref, g_sem
):
    seat = seat_ref[0]
    loads = gathered(core_ref[0], own_in, far_in, g_ref, g_sem)
    share = mine_ref.shape[1]
    half = w_ref.shape[1] // 2
    for m, (old_ref, x) in enumerate(zip((wg_ref, wu_ref, wd_ref), orthogonal(loads))):
        w_ref[m] = moved_weight(old_ref[0], x)
        peer_ref[m] = w_ref[m, pl.ds(pl.multiple_of(seat * share, share), share), :]
        mine_ref[m] = w_ref[m, pl.ds(pl.multiple_of(half + seat * share, share), share), :]


def last_update(core, seat, own, far, weights, share):
    blocks, _, step, features = own.shape
    shape = jax.ShapeDtypeStruct((3, share, features), BF16)
    return pl.pallas_call(
        last_kernel,
        out_shape=(shape, shape),
        in_specs=[SMEM, SMEM] + [VMEM] * 5,
        out_specs=(VMEM, VMEM),
        scratch_shapes=[
            pltpu.VMEM((3, 2, blocks, step, features), BF16),
            pltpu.VMEM((3, features, features), BF16),
            pltpu.SemaphoreType.DMA((6,)),
        ],
        compiler_params=ROOM,
    )(core, seat, own, far, *weights)


def blocks_of(place, wo_in, wo_ref, sem):
    x_ref, masks, line = place
    columns = wo_ref.shape[2]
    loads = []
    for i, (group, mask) in enumerate(masks):
        block = line * group + jnp.bitwise_xor(x_ref[0], mask)
        columns_of = pl.ds(pl.multiple_of(block * columns, 128), columns)
        loads.append(start(wo_in.at[:, columns_of], wo_ref.at[i], sem.at[i]))
    return loads


def products(rows, loads, wo_ref, a_ref, b_ref):
    for i in range(4):
        loads[i].wait()
        (a_ref, b_ref)[i // 2][i % 2] = nn(rows, wo_ref[i]).astype(BF16)


def first_products_kernel(
    masks, line, x_ref, q_in, wg_ref, wu_ref, wd_ref, wo_in, a_ref, b_ref, rows_ref, q_ref, wo_ref, sem, wo_sem
):
    query = start(q_in, q_ref, sem)
    loads = blocks_of((x_ref, masks, line), wo_in, wo_ref, wo_sem)
    query.wait()
    q = q_ref[...]
    x = nn(q, wg_ref[0])
    act = (jax.nn.silu(x) * nn(q, wu_ref[0])).astype(BF16)
    raw = nn(act, wd_ref[0])
    rows = (raw * lax.rsqrt(jnp.mean(raw * raw, axis=-1, keepdims=True) + 1e-6)).astype(BF16)
    rows_ref[...] = rows
    products(rows, loads, wo_ref, a_ref, b_ref)


def later_products_kernel(masks, line, x_ref, rows_ref, wo_in, a_ref, b_ref, wo_ref, wo_sem):
    loads = blocks_of((x_ref, masks, line), wo_in, wo_ref, wo_sem)
    products(rows_ref[...], loads, wo_ref, a_ref, b_ref)


def first_products(masks, line, x, q, weights, w_out, heads):
    rows, features = q.shape
    columns = w_out.shape[1] // heads
    pair = pltpu.VMEM((2, rows, columns), BF16)
    return pl.pallas_call(
        functools.partial(first_products_kernel, masks, line),
        out_shape=(pair, pair, pltpu.VMEM((rows, features), BF16)),
        in_specs=[SMEM, HBM, VMEM, VMEM, VMEM, HBM],
        out_specs=(VMEM,) * 3,
        scratch_shapes=[
            pltpu.VMEM((rows, features), BF16),
            pltpu.VMEM((4, features, columns), BF16),
            pltpu.SemaphoreType.DMA,
            pltpu.SemaphoreType.DMA((4,)),
        ],
        compiler_params=ROOM,
    )(x, q, *weights, w_out)


def later_products(masks, line, x, rows, w_out, heads):
    features = rows.shape[1]
    columns = w_out.shape[1] // heads
    pair = pltpu.VMEM((2, rows.shape[0], columns), BF16)
    return pl.pallas_call(
        functools.partial(later_products_kernel, masks, line),
        out_shape=(pair, pair),
        in_specs=[SMEM, VMEM, HBM],
        out_specs=(VMEM, VMEM),
        scratch_shapes=[pltpu.VMEM((4, features, columns), BF16), pltpu.SemaphoreType.DMA((4,))],
        compiler_params=ROOM,
    )(x, rows, w_out)


def halve_kernel(a_ref, ar_ref, b_ref, br_ref, a_keep, a_send, b_keep, b_send):
    for kept, come, keep, send in ((a_ref, ar_ref, a_keep, a_send), (b_ref, br_ref, b_keep, b_send)):
        keep[...] = (kept[0].astype(F32) + come[0].astype(F32)).astype(BF16)
        send[...] = (kept[1].astype(F32) + come[1].astype(F32)).astype(BF16)


def halve(a, a_come, b, b_come):
    return call(halve_kernel, (pltpu.HBM(a.shape[1:], BF16),) * 4, (a, a_come, b, b_come))


def choose_kernel(far_ref, a_ref, ar_ref, b_ref, br_ref, keep_ref, send_ref):
    a = (a_ref[...].astype(F32) + ar_ref[...].astype(F32)).astype(BF16)
    b = (b_ref[...].astype(F32) + br_ref[...].astype(F32)).astype(BF16)
    second = far_ref[0] == 1
    keep_ref[...] = jnp.where(second, b, a)
    send_ref[...] = jnp.where(second, a, b)


def choose(far, a, a_come, b, b_come):
    return call(choose_kernel, (pltpu.HBM(a.shape, BF16),) * 2, (far, a, a_come, b, b_come), smem=1)


def attend_kernel(position_ref, q_ref, k_ref, v_ref, kp_ref, vp_ref, out_ref):
    rows = q_ref.shape[0]
    has_prior = position_ref[0] > 0
    row = lax.broadcasted_iota(jnp.int32, (rows, rows), 0)
    column = lax.broadcasted_iota(jnp.int32, (rows, rows), 1)
    here = column <= row
    for h in range(q_ref.shape[1] // AD):
        cols = slice(h * AD, (h + 1) * AD)
        q = q_ref[:, cols]
        now = nt(q, k_ref[:, cols])
        before = nt(q, kp_ref[:, cols])
        before = jnp.where(has_prior, before * AD**-0.5, -1e30)
        scores = jnp.where(here, now * AD**-0.5, before)
        e = jnp.exp(scores - jnp.max(scores, axis=-1, keepdims=True))
        probs = e / jnp.sum(e, axis=-1, keepdims=True)
        probs_now = jnp.where(here, probs, 0.0).astype(BF16)
        probs_before = jnp.where(here, 0.0, probs).astype(BF16)
        out_ref[:, cols] = nn(probs_now, v_ref[:, cols]) + nn(probs_before, vp_ref[:, cols])


def attend(position, q, k, v, k_prior, v_prior):
    return call(
        attend_kernel, pltpu.VMEM(q.shape, F32), (position, q, k, v, k_prior, v_prior), smem=1
    )


def swap(x, axis):
    return lax.ppermute(x, axis, [(0, 1), (1, 0)])


def half_sum_kernel(own_ref, come_ref, out_ref):
    for j in range(own_ref.shape[0]):
        out_ref[j] = (own_ref[j].astype(F32) + come_ref[j].astype(F32)).astype(BF16)


def half_sum(own, come):
    return call(half_sum_kernel, pltpu.VMEM(own.shape, BF16), (own, near(come)))


def share_kernel(parts_ref, *out_refs):
    total = parts_ref[0].astype(F32)
    for j in range(1, parts_ref.shape[0]):
        total += parts_ref[j].astype(F32)
    total = total.astype(BF16)
    (out_ref,) = out_refs
    if out_ref.shape == total.shape:
        out_ref[...] = total
    else:
        for j in range(out_ref.shape[0]):
            out_ref[j] = total


def exchanged(blocks):
    return lax.all_to_all(blocks, CHIPS, 0, 0, tiled=True)


def share_of(parts, spread):
    shape = parts.shape if spread else parts.shape[1:]
    return call(share_kernel, pltpu.VMEM(shape, BF16), (near(parts),))


def copies_kernel(share_ref, out_ref):
    for j in range(out_ref.shape[0]):
        out_ref[j] = share_ref[...]


def copies_of(share):
    return call(copies_kernel, pltpu.VMEM((lax.axis_size(CHIPS), *share.shape), BF16), (near(share),))


def near(x):
    return pltpu.with_memory_space_constraint(x, pltpu.VMEM)


def stored(x):
    return pltpu.with_memory_space_constraint(x, pltpu.HBM)


def together(*arrays):
    return lax.optimization_barrier(arrays)


def flip(x, mask):
    devices = range(lax.axis_size(HEAD[1]))
    return lax.ppermute(x, HEAD[1], [(i, i ^ mask) for i in devices])


def on_device(fast_q, fast_k, fast_v, rates, w_gate, w_up, w_down, w_out, att_q, att_k, att_v):
    chips = lax.axis_size(CHIPS)
    heads = lax.axis_size(HEAD)
    core = lax.axis_index("core").astype(jnp.int32).reshape(1)
    seat = lax.axis_index(SEQ[1:]).astype(jnp.int32).reshape(1)
    span = lax.axis_index("span")
    position = lax.axis_index(SEQ).astype(jnp.int32).reshape(1)
    seats = lax.axis_size(SEQ)
    far = lax.axis_index(HEAD[0]).astype(jnp.int32).reshape(1)
    x = lax.axis_index(HEAD[1]).astype(jnp.int32).reshape(1)
    line = lax.axis_size(HEAD[1])
    fast_q, fast_k, fast_v, rates, w_out = map(stored, (fast_q, fast_k, fast_v, rates, w_out))
    weights = tuple(map(stored, (w_gate, w_up, w_down)))

    route = [(i, i + 1) for i in range(seats - 1)]
    k_prior = lax.ppermute(stored(att_k), SEQ, route)
    v_prior = lax.ppermute(stored(att_v), SEQ, route)

    own, away = gradients(core, fast_k, fast_v, rates, weights, chips)
    share = share_of(exchanged(half_sum(own, swap(away, "core"))), False)
    given = lax.ppermute(share, "span", [(0, 1)])
    k_prior, v_prior, share = together(k_prior, v_prior, share)
    attended = attend(position, att_q, att_k, att_v, near(k_prior), near(v_prior))
    given, attended = together(given, attended)
    own = exchanged(copies_of(given))
    weights, own, away = update(core, rates, near(own), near(swap(own, "core")), weights, fast_k, fast_v)

    sent = ((0, 1), (0, 2), (1, 3), (1, 2))
    held = ((0, 0), (0, 3), (1, 0), (1, 1))
    come = swap(away, "core")
    a_sent, b_sent, rows = first_products(sent, line, x, fast_q, weights, w_out, heads)
    come, a_sent, b_sent, rows = together(come, a_sent, b_sent, rows)
    a_come = flip(a_sent, 1)
    b_come = flip(b_sent, 3)
    a_held, b_held = later_products(held, line, x, rows, w_out, heads)
    half = half_sum(own, come)
    parts = exchanged(half)
    a_held, a_sent, b_held, b_sent = halve(a_held, a_come, b_held, b_come)
    a_come = flip(a_sent, 3)
    b_come = flip(b_sent, 1)
    copies = share_of(parts, True)
    own = exchanged(copies)
    held, sent = choose(far, a_held, a_come, b_held, b_come)
    come = swap(sent, HEAD[0])
    away = swap(own, "core")

    mine, peer = last_update(core, seat, near(own), near(away), weights, w_gate.shape[1] // seats)
    given = lax.ppermute(peer, "span", [(1, 0)])
    final = jnp.where(span == 1, mine, given)[:, None]
    mixed = (attended + held.astype(F32) + come.astype(F32)).astype(BF16)
    return mixed, final


def solution(mesh):
    split = Mesh(mesh.devices.reshape(2, 2, 4, 2, 2, 4), (*SEQ, *HEAD))
    in_specs = (
        P(SEQ, HEAD),
        P(SEQ, HEAD),
        P(SEQ, HEAD),
        P(HEAD, SEQ),
        P(HEAD, None, None),
        P(HEAD, None, None),
        P(HEAD, None, None),
        P(HEAD, None),
        P(SEQ, HEAD),
        P(SEQ, HEAD),
        P(SEQ, HEAD),
    )
    out_specs = (P(SEQ, HEAD), P(None, HEAD, SEQ, None))
    return jax.shard_map(on_device, mesh=split, in_specs=in_specs, out_specs=out_specs, check_vma=False)
```
